32 devices in a mesh: rep: 8 (over y, x, core), shard: 4 (over z).
Axes of the slice: x: 2, y: 2, z: 4, core: 2. Of those that a mesh axis runs over, the one named last changes fastest.
Arguments:
- inputs: bfloat16 [8, 2048, 1024], P('rep', 'shard'), may hold values from -6 to 6
- cotangent: bfloat16 [8, 2048, 1024], P('rep', 'shard'), may hold values from -6 to 6
- segments: int32 [8, 2048], P('rep'), may hold values from 0 to 3, never falling along the last dimension, each value on 1 to 1280 neighbouring positions
- master: float32 [17088512], P(('rep', 'shard')), may hold values from -9.22 to 1.3, as said below
- moment_one: float32 [17088512], P(('rep', 'shard')), may hold values from -1.5 to 1.5
- moment_two: float32 [17088512], P(('rep', 'shard')), may hold values from 0.003 to 0.1
Outputs:
- output: bfloat16 [8, 2048, 1024], P('rep', 'shard')
- grad_inputs: bfloat16 [8, 2048, 1024], P('rep', 'shard')
- grad_master: float32 [17088512], P(('rep', 'shard'))
- new_moment_one: float32 [17088512], P(('rep', 'shard'))
- new_moment_two: float32 [17088512], P(('rep', 'shard'))
- update: float32 [17088512], P(('rep', 'shard'))
- grad_norm: float32 [], replicated
The draws below stay inside these ranges and needn't reach their ends.
Inputs may be any that keep to these rules, and one draw needn't show every extreme that they name: `master`: the block's parameters laid out as the first step lists them; entries from 17074448 on are unused. `segments`: in each sequence document numbers start at 0 and never fall.
All inputs are finite; a program needn't handle non-finite values.
Results may differ from the reference program's by a relative error of at most 0.014.
The reference program's roundings to bfloat16 on the way count: a program that leaves them out, or rounds other values in their place, can miss the bound.
Values may be sent and summed in bfloat16 or wider, within the bound.
No kernel may reach another device: no remote copies, remote signals or barrier semaphores. Data moves between devices by JAX's collectives and lax.ppermute only.
A program may use at most 384 MiB of HBM per device.

```python
import math
import jax
import jax.numpy as jnp
import numpy as np
from jax import lax

D = 1024
NH = 8
DK = 128
DV = 256
FF = 2816
CONV = 4
SPAN = 64
SEQLEN = 2048
DOCS = 4
STEP = 10
DOCMAX = 1280
PARAMS = 17074448
NFLAT = 17088512
SEQS = 8


def layout_drawn():
    key_width = NH * DK
    value_width = NH * DV
    return [('norm_in', (D,)), ('w_query', (D, key_width)), ('w_key', (D, key_width)), ('w_value', (D, value_width)), ('w_gate', (D, value_width)), ('w_decay', (D, NH)), ('w_beta', (D, NH)), ('decay_log', (NH,)), ('decay_bias', (NH,)), ('conv_query', (CONV, key_width)), ('conv_key', (CONV, key_width)), ('conv_value', (CONV, value_width)), ('norm_head', (DV,)), ('w_out', (value_width, D)), ('norm_ffn', (D,)), ('w_ffgate', (D, FF)), ('w_ffup', (D, FF)), ('w_ffdown', (FF, D))]


def draw_master(key, part):
    pieces = []
    position = 0
    for param_name, arr_dims in layout_drawn():
        entries = math.prod(arr_dims)
        unit = jax.random.uniform(jax.random.fold_in(key, position + 11), (entries,), jnp.float32, -1.0, 1.0)
        position += 1
        prefix = param_name[:4]
        if prefix == 'norm':
            piece = 1.0 + 0.3 * unit
        elif param_name == 'decay_log':
            lower_end = math.log(0.001)
            upper_end = math.log(0.05)
            piece = lower_end + (upper_end - lower_end) * 0.5 * (unit + 1.0)
        elif param_name == 'decay_bias':
            piece = unit
        elif prefix == 'conv':
            piece = 0.6 * unit
        else:
            factor = 1.0
            if param_name == 'w_out':
                factor = 1.5
            if param_name == 'w_ffdown':
                factor = 2.0
            piece = unit * factor * math.sqrt(3.0 / arr_dims[0])
        pieces.append(piece)
    spare = jax.random.uniform(jax.random.fold_in(key, 97), (NFLAT - PARAMS,), jnp.float32, -0.01, 0.01)
    pieces.append(spare)
    return jnp.concatenate(pieces).astype(jnp.float32)


def level_of(own_key, dims, shards, least, top_value):
    gain, own = 1.0, jax.random.fold_in(own_key, 6)
    for dim, parts in shards:
        draws = jnp.exp(jax.random.uniform(jax.random.fold_in(own, dim), (parts,), jnp.float32, least / len(shards), top_value / len(shards)))
        gain = gain * jnp.repeat(draws, dims[dim] // parts).reshape([-1 if axis == dim else 1 for axis in range(len(dims))])
    return gain


def length_profile(amount, total, limit, lean):
    loads = [(1 << 20) // math.isqrt(rank ** lean) + 1 for rank in range(2, amount + 1)]
    rest, holding = total - limit - (amount - 1), [1] * (amount - 1)
    while rest > 0:
        candidates = [i for i in range(amount - 1) if holding[i] < limit]
        pool, left = sum([loads[i] for i in candidates]), rest
        for i in candidates:
            addition = min(limit - holding[i], max(1, left * loads[i] // pool), rest)
            holding[i] = holding[i] + addition
            rest = rest - addition
    return np.array([limit] + holding)


def uneven_parts(stream_key, number_of, total, bound, slope):
    if number_of == 2:
        one = jax.random.randint(stream_key, (), max(1, total - bound), min(bound, total - 1) + 1)
        return jnp.stack([one, total - one])
    sizes = jnp.asarray(length_profile(number_of, total, bound, slope), jnp.int32)
    twos = (number_of - 1) // 2
    donor, sink = sizes[1:1 + 2 * twos:2], sizes[2:2 + 2 * twos:2]
    room = jnp.minimum(donor - 1, bound - sink)
    shifted = jax.random.randint(jax.random.fold_in(stream_key, 1), (twos,), 0, 1 << 20) % (room + 1)
    sizes = sizes.at[1:1 + 2 * twos:2].set(donor - shifted).at[2:2 + 2 * twos:2].set(sink + shifted)
    return sizes[jax.random.permutation(jax.random.fold_in(stream_key, 2), number_of)]


def normal_values(stream_key, extent, width, bound, shards=(), kind=jnp.bfloat16):
    drawn = jax.random.normal(stream_key, extent, jnp.float32) * width
    if len(shards) > 0:
        drawn = level_of(stream_key, extent, shards, -0.22, 0.18) * drawn
    return jnp.clip(drawn, min=-bound, max=bound).astype(kind)


def setup_inputs(seed: int = 0) -> dict:
    keys = jax.random.split(jax.random.key(seed), 7)
    return {
        "inputs": normal_values(keys[0], (SEQS, SEQLEN, D), 1.0, 6.0, ((0, 8), (1, 4))),
        "cotangent": normal_values(keys[1], (SEQS, SEQLEN, D), 1.0, 6.0, ((0, 8), (1, 4))),
        "segments": jax.vmap(lambda own: jnp.searchsorted(jnp.cumsum(uneven_parts(own, DOCS, SEQLEN, DOCMAX, 0)), jnp.arange(SEQLEN), side="right"))(jax.random.split(keys[2], SEQS)).reshape((SEQS, SEQLEN)).astype(jnp.int32),
        "master": draw_master(jax.random.fold_in(keys[6], 71), 0),
        "moment_one": normal_values(keys[4], (NFLAT,), 0.1, 1.5, ((0, 32),), jnp.float32),
        "moment_two": jnp.clip(jnp.exp(math.log(0.1) - 3.506558 * jax.random.uniform(keys[5], (NFLAT,), jnp.float32) ** level_of(keys[5], (NFLAT,), ((0, 32),), -0.2, 0.2)), 0.003, 0.1),
    }


EPS_NORM = 1e-06
LEARN_RATE = 0.01
BETA_ONE = 0.9
BETA_TWO = 0.95
ADAM_EPS = 1e-08
DECAY_RATE = 0.1
PRECISE = lax.Precision.HIGHEST

@jax.custom_vjp
def low(v):
    return lax.optimization_barrier(v.astype(jnp.bfloat16)).astype(jnp.float32)

@jax.custom_vjp
def low_back(v):
    return v

def low_keep(v):
    return (low(v), None)

def low_pass(kept, grad):
    return (grad,)

def back_keep(v):
    return (v, None)

def back_low(kept, grad):
    return (low(grad),)
low.defvjp(low_keep, low_pass)
low_back.defvjp(back_keep, back_low)

def layout():
    key_width = NH * DK
    value_width = NH * DV
    return [('norm_in', (D,)), ('w_query', (D, key_width)), ('w_key', (D, key_width)), ('w_value', (D, value_width)), ('w_gate', (D, value_width)), ('w_decay', (D, NH)), ('w_beta', (D, NH)), ('decay_log', (NH,)), ('decay_bias', (NH,)), ('conv_query', (CONV, key_width)), ('conv_key', (CONV, key_width)), ('conv_value', (CONV, value_width)), ('norm_head', (DV,)), ('w_out', (value_width, D)), ('norm_ffn', (D,)), ('w_ffgate', (D, FF)), ('w_ffup', (D, FF)), ('w_ffdown', (FF, D))]

def unpack(flat_vec):
    result = {}
    offset = 0
    for param_name, arr_dims in layout():
        entries = math.prod(arr_dims)
        result[param_name] = flat_vec[offset:offset + entries].reshape(arr_dims)
        offset += entries
    return result

def product(mat_left, mat_right):
    return jnp.dot(mat_left, mat_right, precision=PRECISE)

def rms_norm(row_vals, gain_vals):
    return row_vals * lax.rsqrt(lax.optimization_barrier(jnp.mean(row_vals * row_vals, -1, keepdims=True)) + EPS_NORM) * gain_vals

def swiglu(gate_vals, up_vals):
    return jax.nn.silu(gate_vals) * up_vals

def short_conv(ext_rows, conv_weights, ext_segs):
    length = ext_rows.shape[0] - (CONV - 1)
    own_segs = ext_segs[CONV - 1:]
    summed = jnp.zeros((length, ext_rows.shape[1]), jnp.float32)
    for lag_step in range(CONV):
        start_row = CONV - 1 - lag_step
        same_seg = (ext_segs[start_row:start_row + length] == own_segs).astype(jnp.float32)
        summed = summed + conv_weights[lag_step][None, :] * ext_rows[start_row:start_row + length] * same_seg[:, None]
    return jax.nn.silu(summed)

def mixer_inputs(ext_query, ext_key, ext_value, decay_in, beta_in, conv_query, conv_key, conv_value, decay_log, decay_bias, ext_segs):
    length = decay_in.shape[0]
    queries = short_conv(ext_query, conv_query, ext_segs).reshape(length, NH, DK)
    queries = queries * lax.rsqrt(lax.optimization_barrier(jnp.sum(queries * queries, -1, keepdims=True)) + EPS_NORM) * DK ** (-0.5)
    key_vecs = short_conv(ext_key, conv_key, ext_segs).reshape(length, NH, DK)
    key_vecs = key_vecs * lax.rsqrt(lax.optimization_barrier(jnp.sum(key_vecs * key_vecs, -1, keepdims=True)) + EPS_NORM)
    values = short_conv(ext_value, conv_value, ext_segs).reshape(length, NH, DV)
    betas = jax.nn.sigmoid(beta_in)
    gains_log = -jnp.exp(decay_log)[None, :] * jax.nn.softplus(decay_in + decay_bias[None, :])
    return (queries, key_vecs, values, betas, gains_log)

def delta_span(state, block_in):
    queries, key_vecs, values, betas, gains_log, seg_ids, prev_seg = block_in
    block_len = seg_ids.shape[0]
    cumul = jnp.cumsum(gains_log, axis=0)
    positions = jnp.arange(block_len)
    same_doc = seg_ids[:, None] == seg_ids[None, :]
    allowed = (same_doc & (positions[:, None] >= positions[None, :])).astype(jnp.float32)
    strict = (positions[:, None] > positions[None, :]).astype(jnp.float32)
    log_gaps = cumul[:, None, :] - cumul[None, :, :]
    decay_mat = jnp.exp(jnp.where(allowed[:, :, None] > 0.5, log_gaps, 0.0)) * allowed[:, :, None]
    decay_mat = jnp.transpose(decay_mat, (2, 0, 1))
    incoming = (seg_ids == prev_seg).astype(jnp.float32)[:, None] * jnp.exp(cumul)
    key_gram = jnp.einsum('thd,shd->hts', key_vecs, key_vecs, precision=PRECISE)
    system = jnp.eye(block_len, dtype=jnp.float32)[None] + jnp.transpose(betas)[:, :, None] * key_gram * decay_mat * strict[None]
    key_state = jnp.einsum('thd,hde->the', key_vecs, state, precision=PRECISE)
    rhs_vals = betas[:, :, None] * (values - incoming[:, :, None] * key_state)
    rhs_vals = jnp.transpose(rhs_vals, (1, 0, 2))
    deltas = lax.linalg.triangular_solve(system, rhs_vals, left_side=True, lower=True, unit_diagonal=True)
    query_key = jnp.einsum('thd,shd->hts', queries, key_vecs, precision=PRECISE) * decay_mat
    outputs = incoming[:, :, None] * jnp.einsum('thd,hde->the', queries, state, precision=PRECISE)
    outputs = outputs + jnp.einsum('hts,hse->the', query_key, deltas, precision=PRECISE)
    last_decay = decay_mat[:, block_len - 1, :]
    new_state = incoming[block_len - 1][:, None, None] * state
    new_state = new_state + jnp.einsum('shd,hs,hse->hde', key_vecs, last_decay, deltas, precision=PRECISE)
    return (new_state, outputs)

def delta_run(queries, key_vecs, values, betas, gains_log, seg_ids, prev_seg, state):
    total_len = seg_ids.shape[0]
    blocks = total_len // SPAN

    def split_blocks(array_in):
        return array_in.reshape((blocks, SPAN) + array_in.shape[1:])
    seg_blocks = split_blocks(seg_ids)
    prev_list = jnp.concatenate([jnp.reshape(prev_seg, (1,)).astype(jnp.int32), seg_blocks[:-1, SPAN - 1].astype(jnp.int32)])
    final_state, outputs = lax.scan(jax.checkpoint(delta_span), state, (split_blocks(queries), split_blocks(key_vecs), split_blocks(values), split_blocks(betas), split_blocks(gains_log), seg_blocks, prev_list))
    return (outputs.reshape((total_len,) + outputs.shape[2:]), final_state)

def gated_norm(mixed, gate_raw, norm_head):
    length = mixed.shape[0]
    normed_heads = rms_norm(mixed, norm_head).reshape(length, NH * DV)
    return normed_heads * jax.nn.silu(gate_raw)

def pad_front(row_vals):
    return jnp.concatenate([jnp.zeros((CONV - 1, row_vals.shape[1]), jnp.float32), row_vals], 0)

def layer_forward(flat_vec, in_rows, seg_ids):
    params = unpack(low(flat_vec))
    normed = low(rms_norm(in_rows, params['norm_in']))
    proj_query = low(low_back(product(normed, params['w_query'])))
    proj_key = low(low_back(product(normed, params['w_key'])))
    proj_value = low(low_back(product(normed, params['w_value'])))
    gate_raw = low_back(product(normed, params['w_gate']))
    decay_raw = low_back(product(normed, params['w_decay']))
    beta_raw = low_back(product(normed, params['w_beta']))
    ext_segs = jnp.concatenate([jnp.full((CONV - 1,), -1, jnp.int32), seg_ids.astype(jnp.int32)])
    queries, key_vecs, values, betas, gains_log = mixer_inputs(pad_front(proj_query), pad_front(proj_key), pad_front(proj_value), decay_raw, beta_raw, params['conv_query'], params['conv_key'], params['conv_value'], params['decay_log'], params['decay_bias'], ext_segs)
    start_state = jnp.zeros((NH, DK, DV), jnp.float32)
    mixed, leftover = delta_run(queries, key_vecs, values, betas, gains_log, seg_ids.astype(jnp.int32), jnp.array(-1, jnp.int32), start_state)
    gated = low(gated_norm(mixed, gate_raw, params['norm_head']))
    branch = low_back(product(gated, params['w_out']))
    middle = in_rows + branch
    normed_two = low(rms_norm(middle, params['norm_ffn']))
    ff_gate = low_back(product(normed_two, params['w_ffgate']))
    ff_up = low_back(product(normed_two, params['w_ffup']))
    hidden = low(swiglu(ff_gate, ff_up))
    return middle + product(hidden, params['w_ffdown'])

def reference(inputs, cotangent, segments, master, moment_one, moment_two):
    flat_vec = master.astype(jnp.float32)

    def per_sequence(grad_total, seq_item):
        seq_in, seq_cot, seq_seg = seq_item

        def forward_fn(flat_arg, in_arg):
            return layer_forward(flat_arg, in_arg, seq_seg)
        out_vals, pullback = jax.vjp(forward_fn, flat_vec, seq_in.astype(jnp.float32))
        grad_flat, grad_in = pullback(seq_cot.astype(jnp.float32))
        return (grad_total + grad_flat, (out_vals.astype(jnp.bfloat16), grad_in.astype(jnp.bfloat16)))
    grad_total, (outputs, grad_inputs) = lax.scan(per_sequence, jnp.zeros((NFLAT,), jnp.float32), (inputs, cotangent, segments))
    grad_norm = jnp.sqrt(jnp.sum(grad_total * grad_total))
    clip_scale = jnp.minimum(1.0, math.sqrt(PARAMS) / (grad_norm + 1e-06))
    clipped = grad_total * clip_scale
    new_one = BETA_ONE * moment_one + (1.0 - BETA_ONE) * clipped
    new_two = BETA_TWO * moment_two + (1.0 - BETA_TWO) * clipped * clipped
    fix_one = 1.0 - BETA_ONE ** STEP
    fix_two = 1.0 - BETA_TWO ** STEP
    update = -LEARN_RATE * (new_one / fix_one / (jnp.sqrt(new_two / fix_two) + ADAM_EPS) + DECAY_RATE * master)
    return (outputs, grad_inputs, grad_total, new_one, new_two, update, grad_norm)
```

```python
import math

import jax
import jax.numpy as jnp
from jax import lax
from jax.experimental import pallas as pl
from jax.experimental.pallas import tpu as pltpu
from jax.sharding import PartitionSpec as P

D = 1024
FF = 2816
STEP = 10
PARAMS = 17074448
NFLAT = 17088512
LEARN_RATE = 0.01
BETA_ONE = 0.9
BETA_TWO = 0.95
ADAM_EPS = 1e-08
DECAY_RATE = 0.1
AXES = ("rep", "shard")


NH=8; DK=128; DV=256; CONV=4; CH=128; HG=4
EPS_NORM=1e-6
bf=jnp.bfloat16; f32=jnp.float32

def mm(a,b): return lax.dot_general(a.astype(bf),b.astype(bf),(((1,),(0,)),((),())),preferred_element_type=f32)
def mmt(a,b): return lax.dot_general(a.astype(bf),b.astype(bf),(((1,),(1,)),((),())),preferred_element_type=f32)
def tmm(a,b): return lax.dot_general(a.astype(bf),b.astype(bf),(((0,),(0,)),((),())),preferred_element_type=f32)
def split(a):
    h=a.astype(bf)
    return h,(a-h.astype(f32)).astype(bf)
def mm3(a,b):
    (ah,al),(bh,bl)=a,b
    return mm(ah,bh)+(mm(ah,bl)+mm(al,bh))

C_BETA,C_CUM,C_IN,C_GAM,C_SEG,C_SAME=0,8,16,24,32,32
R_CUM,R_SEG=0,8

def conv_shift(x,prev):
    xe=jnp.concatenate([prev,x],0)
    return [x]+[pltpu.roll(xe,j,0)[8:] for j in range(1,CONV)]

def conv_sum(xs,w,col):
    s=w[0:1]*xs[0]
    for j in range(1,CONV):
        s=s+w[j:j+1]*(xs[j]*col[:,C_SAME+j:C_SAME+j+1])
    return s

def sigmoid(v): return 1.0/(1.0+jnp.exp(-v))

def decay_tile(cum_c,cum_r,seg_c,seg_r,rows,cols):
    keep=(seg_c==seg_r)&(rows>=cols)
    return jnp.where(keep,jnp.exp(jnp.where(keep,cum_c-cum_r,0.0)),0.0)

def prev_rows(chunk,main_ref,halo_ref,lo,hi):
    p=jnp.where(chunk==0,halo_ref[8:16,lo:hi].astype(f32),main_ref[8:16,lo:hi].astype(f32))
    return p

def local_kernel(q_ref,k_ref,v_ref,qp_ref,kp_ref,vp_ref,qh_ref,kh_ref,vh_ref,cq_ref,ck_ref,cv_ref,col_ref,row_ref,
                 qn_ref,kn_ref,t_ref,p_ref,w_ref,u_ref,mloc_ref,nloc_ref,run):
    hg=pl.program_id(0); chunk=pl.program_id(1)
    col=col_ref[0]; row=row_ref[0]
    rows=lax.broadcasted_iota(jnp.int32,(CH,CH),0); cols=lax.broadcasted_iota(jnp.int32,(CH,CH),1)
    eye=(rows==cols).astype(f32)
    seg_c=col[:,C_SEG:C_SEG+1]; seg_r=row[R_SEG:R_SEG+1]
    @pl.when(chunk==0)
    def _():
        for h in range(HG):
            run[h,:,:DK]=eye
            run[h,:,DK:]=jnp.zeros((DK,DV),f32)
    masks=[]
    b=1
    while b<CH:
        lo=((rows//b)%2==1)&((cols//b)==(rows//b)-1)
        masks.append(lo); b*=2
    kns=[];As=[];ps=[];betas=[];ins=[]
    for h in range(HG):
        a,z=h*DK,(h+1)*DK
        xq=conv_shift(q_ref[:,a:z].astype(f32),prev_rows(chunk,qp_ref,qh_ref,a,z))
        sq=conv_sum(xq,cq_ref[:,a:z],col); uq=sq*sigmoid(sq)
        qn=uq*(lax.rsqrt(jnp.sum(uq*uq,-1,keepdims=True)+EPS_NORM)*DK**-0.5)
        xk=conv_shift(k_ref[:,a:z].astype(f32),prev_rows(chunk,kp_ref,kh_ref,a,z))
        sk=conv_sum(xk,ck_ref[:,a:z],col); uk=sk*sigmoid(sk)
        kn=uk*lax.rsqrt(jnp.sum(uk*uk,-1,keepdims=True)+EPS_NORM)
        qn_ref[:,a:z]=qn.astype(bf); kn_ref[:,a:z]=kn.astype(bf)
        beta=col[:,C_BETA+h:C_BETA+h+1]; cum_c=col[:,C_CUM+h:C_CUM+h+1]; cum_r=row[R_CUM+h:R_CUM+h+1]
        d=decay_tile(cum_c,cum_r,seg_c,seg_r,rows,cols)
        kk=mm3(split(kn),tuple(s for s in split(kn))) if False else mmt(kn,kn)
        As.append(jnp.where(rows>cols,beta*kk*d,0.0))
        p=mmt(qn,kn)*d
        p_ref[:,a:z]=p.astype(bf)
        kns.append(kn); betas.append(beta); ins.append(col[:,C_IN+h:C_IN+h+1])
    asp=[split(A) for A in As]
    ts=[eye-jnp.where(masks[0],A,0.0) for A in As]
    zero=jnp.zeros((CH,CH),bf)
    for m in masks[1:]:
        tsp=[split(t) for t in ts]
        xs=[mm3((jnp.where(m,ah,zero),jnp.where(m,al,zero)),tp) for (ah,al),tp in zip(asp,tsp)]
        xsp=[split(x) for x in xs]
        ts=[t-mm3(tp,xp) for t,tp,xp in zip(ts,tsp,xsp)]
    for h in range(HG):
        a,z=h*DK,(h+1)*DK
        va,vz=h*DV,(h+1)*DV
        t=ts[h]; t_ref[:,a:z]=t.astype(bf)
        xv=conv_shift(v_ref[:,va:vz].astype(f32),prev_rows(chunk,vp_ref,vh_ref,va,vz))
        sv=conv_sum(xv,cv_ref[:,va:vz],col); v=sv*sigmoid(sv)
        u=mm(t,betas[h]*v); w=mm(t,(betas[h]*ins[h])*kns[h])
        u_ref[:,va:vz]=u; wb=w.astype(bf); w_ref[:,a:z]=wb
        gam=col[:,C_GAM+h:C_GAM+h+1]
        r=run[h]
        wr=mm(wb,r)
        delta=jnp.concatenate([-wr[:,:DK],u-wr[:,DK:]],1)
        r=ins[h][CH-1:CH]*r+tmm(gam*kns[h],delta)
        run[h]=r
        @pl.when(chunk==pl.num_programs(1)-1)
        def _():
            mloc_ref[h]=r[:,:DK]; nloc_ref[h]=r[:,DK:]

def local_pass(q,k,v,qh,kh,vh,cq,ck,cv,col,row):
    T=q.shape[0]; n=T//CH
    kw=HG*DK; vw=HG*DV
    def pv(g,c): return (jnp.maximum(c*(CH//16)-1,0),g)
    main=lambda g,c:(c,g)
    halo=lambda g,c:(0,g)
    return pl.pallas_call(local_kernel,grid=(NH//HG,n),
        in_specs=[pl.BlockSpec((CH,kw),main),pl.BlockSpec((CH,kw),main),pl.BlockSpec((CH,vw),main),
                  pl.BlockSpec((16,kw),pv),pl.BlockSpec((16,kw),pv),pl.BlockSpec((16,vw),pv),
                  pl.BlockSpec((16,kw),halo),pl.BlockSpec((16,kw),halo),pl.BlockSpec((16,vw),halo),
                  pl.BlockSpec((CONV,kw),halo),pl.BlockSpec((CONV,kw),halo),pl.BlockSpec((CONV,vw),halo),
                  pl.BlockSpec((1,CH,64),lambda g,c:(g,c,0)),pl.BlockSpec((1,16,CH),lambda g,c:(g,0,c))],
        out_specs=[pl.BlockSpec((CH,kw),main)]*5+[pl.BlockSpec((CH,vw),main),
                  pl.BlockSpec((HG,DK,DK),lambda g,c:(g,0,0)),pl.BlockSpec((HG,DK,DV),lambda g,c:(g,0,0))],
        out_shape=[jax.ShapeDtypeStruct((T,NH*DK),bf)]*5+[jax.ShapeDtypeStruct((T,NH*DV),f32),
                  jax.ShapeDtypeStruct((NH,DK,DK),f32),jax.ShapeDtypeStruct((NH,DK,DV),f32)],
        scratch_shapes=[pltpu.VMEM((HG,DK,DK+DV),f32)],
        compiler_params=pltpu.CompilerParams(dimension_semantics=("arbitrary","arbitrary")),
        cost_estimate=pl.CostEstimate(flops=8*10**9,bytes_accessed=24*2**20,transcendentals=10**6),
        name="delta_local")(q,k,v,q,k,v,qh,kh,vh,cq,ck,cv,col,row)

def mix_kernel(qn_ref,kn_ref,p_ref,w_ref,u_ref,col_ref,s_in_ref,gate_ref,gain_ref,
               mixed_ref,gated_ref,delta_ref,s_ref,state):
    chunk=pl.program_id(1)
    col=col_ref[0]
    @pl.when(chunk==0)
    def _(): state[...]=s_in_ref[...]
    gain=gain_ref[0:1]
    for h in range(HG):
        a,z=h*DK,(h+1)*DK; va,vz=h*DV,(h+1)*DV
        s=state[h]; sb=s.astype(bf)
        s_ref[0,h]=sb
        inn=col[:,C_IN+h:C_IN+h+1]; gam=col[:,C_GAM+h:C_GAM+h+1]
        delta=u_ref[:,va:vz]-mm(w_ref[:,a:z],sb)
        db=delta.astype(bf); delta_ref[:,va:vz]=db
        o=inn*mm(qn_ref[:,a:z],sb)+mm(p_ref[:,a:z],db)
        state[h]=inn[CH-1:CH]*s+tmm(gam*kn_ref[:,a:z].astype(f32),db)
        mixed_ref[:,va:vz]=o
        rs=lax.rsqrt(jnp.mean(o*o,-1,keepdims=True)+EPS_NORM)
        g=gate_ref[:,va:vz].astype(f32)
        gated_ref[:,va:vz]=(o*rs*gain*(g*sigmoid(g))).astype(bf)

def mix_pass(qn,kn,p,w,u,col,s_in,gate,gain):
    T=qn.shape[0]; n=T//CH; kw=HG*DK; vw=HG*DV
    main=lambda g,c:(c,g)
    return pl.pallas_call(mix_kernel,grid=(NH//HG,n),
        in_specs=[pl.BlockSpec((CH,kw),main)]*4+[pl.BlockSpec((CH,vw),main),pl.BlockSpec((1,CH,64),lambda g,c:(g,c,0)),
                  pl.BlockSpec((HG,DK,DV),lambda g,c:(g,0,0)),pl.BlockSpec((CH,vw),main),pl.BlockSpec((8,DV),lambda g,c:(0,0))],
        out_specs=[pl.BlockSpec((CH,vw),main)]*3+[pl.BlockSpec((1,HG,DK,DV),lambda g,c:(c,g,0,0))],
        out_shape=[jax.ShapeDtypeStruct((T,NH*DV),f32),jax.ShapeDtypeStruct((T,NH*DV),bf),jax.ShapeDtypeStruct((T,NH*DV),bf),
                   jax.ShapeDtypeStruct((n,NH,DK,DV),bf)],
        scratch_shapes=[pltpu.VMEM((HG,DK,DV),f32)],
        compiler_params=pltpu.CompilerParams(dimension_semantics=("arbitrary","arbitrary")),
        cost_estimate=pl.CostEstimate(flops=2*10**9,bytes_accessed=24*2**20,transcendentals=10**6),
        name="delta_mix")(qn,kn,p,w,u,col,s_in,gate,gain)

def unmix_kernel(dg_ref,mixed_ref,gate_ref,gain_ref,qn_ref,kn_ref,p_ref,w_ref,col_ref,
                 do_ref,dgate_ref,dgain_ref,e_ref,acc,adj):
    g_id=pl.program_id(0); step=pl.program_id(1); n=pl.num_programs(1)
    col=col_ref[0]; gain=gain_ref[0:1]
    @pl.when(step==0)
    def _(): adj[...]=jnp.zeros_like(adj)
    @pl.when((step==0)&(g_id==0))
    def _(): acc[...]=jnp.zeros_like(acc)
    for h in range(HG):
        a,z=h*DK,(h+1)*DK; va,vz=h*DV,(h+1)*DV
        o=mixed_ref[:,va:vz]; g=gate_ref[:,va:vz].astype(f32); dy=dg_ref[:,va:vz].astype(f32)
        rs=lax.rsqrt(jnp.mean(o*o,-1,keepdims=True)+EPS_NORM)
        sg=sigmoid(g); si=g*sg
        hat=o*rs
        dn=dy*si
        dgate_ref[:,va:vz]=(dy*(hat*gain)*(sg*(1.0+g*(1.0-sg)))).astype(bf)
        acc[...]+=jnp.sum((dn*hat).reshape(CH//8,8,DV),0)
        dw=dn*gain
        do=rs*(dw-hat*jnp.mean(dw*hat,-1,keepdims=True))
        dob=do.astype(bf); do_ref[:,va:vz]=dob
        inn=col[:,C_IN+h:C_IN+h+1]; gam=col[:,C_GAM+h:C_GAM+h+1]
        x=adj[h]
        dd=tmm(p_ref[:,a:z],dob)+mm(gam*kn_ref[:,a:z].astype(f32),x)
        adj[h]=inn[CH-1:CH]*x+tmm(inn*qn_ref[:,a:z].astype(f32),dob)-tmm(w_ref[:,a:z],dd)
    @pl.when(step==n-1)
    def _(): e_ref[...]=adj[...]
    @pl.when((step==n-1)&(g_id==pl.num_programs(0)-1))
    def _(): dgain_ref[...]=acc[...]

def unmix_pass(dgated,mixed,gate,gain,qn,kn,p,w,col):
    T=qn.shape[0]; n=T//CH; kw=HG*DK; vw=HG*DV
    main=lambda g,c:(n-1-c,g)
    return pl.pallas_call(unmix_kernel,grid=(NH//HG,n),
        in_specs=[pl.BlockSpec((CH,vw),main)]*3+[pl.BlockSpec((8,DV),lambda g,c:(0,0))]+[pl.BlockSpec((CH,kw),main)]*4+
                 [pl.BlockSpec((1,CH,64),lambda g,c:(g,n-1-c,0))],
        out_specs=[pl.BlockSpec((CH,vw),main)]*2+[pl.BlockSpec((8,DV),lambda g,c:(0,0)),pl.BlockSpec((HG,DK,DV),lambda g,c:(g,0,0))],
        out_shape=[jax.ShapeDtypeStruct((T,NH*DV),bf)]*2+[jax.ShapeDtypeStruct((8,DV),f32),jax.ShapeDtypeStruct((NH,DK,DV),f32)],
        scratch_shapes=[pltpu.VMEM((8,DV),f32),pltpu.VMEM((HG,DK,DV),f32)],
        compiler_params=pltpu.CompilerParams(dimension_semantics=("arbitrary","arbitrary")),
        cost_estimate=pl.CostEstimate(flops=2*10**9,bytes_accessed=24*2**20,transcendentals=10**6),
        name="delta_unmix")(dgated,mixed,gate,gain,qn,kn,p,w,col)

def conv_back(ds,xs,w,col,carry,first):
    n=ds.shape[1]
    zero=jnp.zeros((8,n),f32)
    total=jnp.concatenate([zero,w[0:1]*ds],0)
    grads=[jnp.sum(ds*xs[0],0,keepdims=True)]
    for j in range(1,CONV):
        dm=ds*col[:,C_SAME+j:C_SAME+j+1]
        grads.append(jnp.sum(dm*xs[j],0,keepdims=True))
        e=jnp.concatenate([zero,w[j:j+1]*dm],0)
        total=total+pltpu.roll(e,CH+8-j,0)
    back=total[:8]
    dp=total[8:]
    dp=jnp.concatenate([dp[:CH-8],dp[CH-8:]+carry],0)
    return dp,back,grads

def silu_back(s):
    sg=sigmoid(s)
    return sg*(1.0+s*(1.0-sg))

def back_kernel(q_ref,k_ref,v_ref,qp_ref,kp_ref,vp_ref,qh_ref,kh_ref,vh_ref,cq_ref,ck_ref,cv_ref,col_ref,row_ref,
                t_ref,p_ref,w_ref,delta_ref,s_ref,do_ref,dend_ref,send_ref,
                dq_ref,dk_ref,dv_ref,bq_ref,bk_ref,bv_ref,tq_ref,tk_ref,tv_ref,gq_ref,gk_ref,gv_ref,dcol_ref,
                adj,cq_c,ck_c,cv_c,s_next):
    step=pl.program_id(1); n=pl.num_programs(1); chunk=n-1-step
    col=col_ref[0]; row=row_ref[0]
    rows=lax.broadcasted_iota(jnp.int32,(CH,CH),0); cols=lax.broadcasted_iota(jnp.int32,(CH,CH),1)
    lane=lax.broadcasted_iota(jnp.int32,(CH,CH),1)
    seg_c=col[:,C_SEG:C_SEG+1]; seg_r=row[R_SEG:R_SEG+1]
    @pl.when(step==0)
    def _():
        adj[...]=dend_ref[...]
        s_next[...]=send_ref[...].astype(bf)
        cq_c[...]=jnp.zeros_like(cq_c); ck_c[...]=jnp.zeros_like(ck_c); cv_c[...]=jnp.zeros_like(cv_c)
        gq_ref[...]=jnp.zeros_like(gq_ref); gk_ref[...]=jnp.zeros_like(gk_ref); gv_ref[...]=jnp.zeros_like(gv_ref)
    dcol=jnp.zeros((CH,CH),f32)
    for h in range(HG):
        a,z=h*DK,(h+1)*DK; va,vz=h*DV,(h+1)*DV
        wq=cq_ref[:,a:z]; wk=ck_ref[:,a:z]; wv=cv_ref[:,va:vz]
        xq=conv_shift(q_ref[:,a:z].astype(f32),prev_rows(chunk,qp_ref,qh_ref,a,z))
        sq=conv_sum(xq,wq,col); uq=sq*sigmoid(sq); rq=lax.rsqrt(jnp.sum(uq*uq,-1,keepdims=True)+EPS_NORM); hq=uq*rq
        qn=hq*DK**-0.5
        xk=conv_shift(k_ref[:,a:z].astype(f32),prev_rows(chunk,kp_ref,kh_ref,a,z))
        sk=conv_sum(xk,wk,col); uk=sk*sigmoid(sk); rk=lax.rsqrt(jnp.sum(uk*uk,-1,keepdims=True)+EPS_NORM); kn=uk*rk
        qb=qn.astype(bf); kb=kn.astype(bf)
        beta=col[:,C_BETA+h:C_BETA+h+1]; cum_c=col[:,C_CUM+h:C_CUM+h+1]; cum_r=row[R_CUM+h:R_CUM+h+1]
        inn=col[:,C_IN+h:C_IN+h+1]; gam=col[:,C_GAM+h:C_GAM+h+1]
        d=decay_tile(cum_c,cum_r,seg_c,seg_r,rows,cols)
        dob=do_ref[:,va:vz]; db=delta_ref[:,va:vz]; sb=s_ref[0,h]
        ds1=adj[h]; ds1b=ds1.astype(bf)
        ddelta=tmm(p_ref[:,a:z],dob)+mm(gam*kn,ds1b)
        ddb=ddelta.astype(bf)
        dr=tmm(t_ref[:,a:z],ddb); drb=dr.astype(bf)
        da=-mmt(drb,db)
        dkk=(jnp.where(rows>cols,da*d,0.0)*beta).astype(bf)
        dqk=(mmt(dob,db)*d).astype(bf)
        dq=inn*mmt(dob,sb)+mm(dqk,kb)
        dkrow=mm(dkk,kb)-(inn*beta)*mmt(drb,sb)
        dkcol=tmm(dqk,qb)+tmm(dkk,kb)+gam*mmt(db,ds1b)
        dv=beta*dr
        dbeta=jnp.sum(dr*db.astype(f32),-1,keepdims=True)*(1.0-beta)
        dg=jnp.sum(qn*dq+kn*(dkrow-dkcol),-1,keepdims=True)
        last=jnp.sum(jnp.sum(ds1*s_next[h].astype(f32),-1,keepdims=True),0,keepdims=True)
        dg=dg+jnp.where(rows[:,:1]==CH-1,last,0.0)
        dcol=jnp.where(lane==h,dbeta,jnp.where(lane==HG+h,dg,dcol))
        adj[h]=inn[CH-1:CH]*ds1+tmm(inn*qn,dob)-tmm(w_ref[:,a:z],ddb)
        s_next[h]=sb
        dy=dq*DK**-0.5
        dsq=rq*(dy-hq*jnp.sum(hq*dy,-1,keepdims=True))*silu_back(sq)
        dk=dkrow+dkcol
        dsk=rk*(dk-kn*jnp.sum(kn*dk,-1,keepdims=True))*silu_back(sk)
        xv=conv_shift(v_ref[:,va:vz].astype(f32),prev_rows(chunk,vp_ref,vh_ref,va,vz))
        sv=conv_sum(xv,wv,col)
        dsv=dv*silu_back(sv)
        for ds,xs,wc,car,out,bref,tref,gref,lo,hi in ((dsq,xq,wq,cq_c,dq_ref,bq_ref,tq_ref,gq_ref,a,z),(dsk,xk,wk,ck_c,dk_ref,bk_ref,tk_ref,gk_ref,a,z),
                                            (dsv,xv,wv,cv_c,dv_ref,bv_ref,tv_ref,gv_ref,va,vz)):
            dp,back,grads=conv_back(ds,xs,wc,col,car[:,lo:hi],None)
            out[:,lo:hi]=dp.astype(bf)
            car[:,lo:hi]=back
            bref[:,lo:hi]=back
            for j in range(CONV):
                gref[j:j+1,lo:hi]+=grads[j]
            @pl.when(step==0)
            def _(): tref[:,lo:hi]=dp[CH-8:]
    dcol_ref[0]=dcol

def back_pass(q,k,v,qh,kh,vh,cq,ck,cv,col,row,t,p,w,delta,s,do,dend,send):
    T=q.shape[0]; n=T//CH; kw=HG*DK; vw=HG*DV
    def pv(g,c): return (jnp.maximum((n-1-c)*(CH//16)-1,0),g)
    main=lambda g,c:(n-1-c,g)
    halo=lambda g,c:(0,g)
    st=pl.BlockSpec((HG,DK,DV),lambda g,c:(g,0,0))
    return pl.pallas_call(back_kernel,grid=(NH//HG,n),
        in_specs=[pl.BlockSpec((CH,kw),main),pl.BlockSpec((CH,kw),main),pl.BlockSpec((CH,vw),main),
                  pl.BlockSpec((16,kw),pv),pl.BlockSpec((16,kw),pv),pl.BlockSpec((16,vw),pv),
                  pl.BlockSpec((16,kw),halo),pl.BlockSpec((16,kw),halo),pl.BlockSpec((16,vw),halo),
                  pl.BlockSpec((CONV,kw),halo),pl.BlockSpec((CONV,kw),halo),pl.BlockSpec((CONV,vw),halo),
                  pl.BlockSpec((1,CH,64),lambda g,c:(g,n-1-c,0)),pl.BlockSpec((1,16,CH),lambda g,c:(g,0,n-1-c)),
                  pl.BlockSpec((CH,kw),main),pl.BlockSpec((CH,kw),main),pl.BlockSpec((CH,kw),main),pl.BlockSpec((CH,vw),main),
                  pl.BlockSpec((1,HG,DK,DV),lambda g,c:(n-1-c,g,0,0)),pl.BlockSpec((CH,vw),main),st,st],
        out_specs=[pl.BlockSpec((CH,kw),main),pl.BlockSpec((CH,kw),main),pl.BlockSpec((CH,vw),main)]+
                  [pl.BlockSpec((8,kw),halo),pl.BlockSpec((8,kw),halo),pl.BlockSpec((8,vw),halo)]*3+
                  [pl.BlockSpec((1,CH,CH),lambda g,c:(g,n-1-c,0))],
        out_shape=[jax.ShapeDtypeStruct((T,NH*DK),bf)]*2+[jax.ShapeDtypeStruct((T,NH*DV),bf)]+
                  [jax.ShapeDtypeStruct((8,NH*DK),f32),jax.ShapeDtypeStruct((8,NH*DK),f32),jax.ShapeDtypeStruct((8,NH*DV),f32)]*3+
                  [jax.ShapeDtypeStruct((NH//HG,T,CH),f32)],
        scratch_shapes=[pltpu.VMEM((HG,DK,DV),f32),pltpu.VMEM((8,kw),f32),pltpu.VMEM((8,kw),f32),pltpu.VMEM((8,vw),f32),pltpu.VMEM((HG,DK,DV),bf)],
        compiler_params=pltpu.CompilerParams(dimension_semantics=("arbitrary","arbitrary")),
        cost_estimate=pl.CostEstimate(flops=4*10**9,bytes_accessed=32*2**20,transcendentals=2*10**6),
        name="delta_back")(q,k,v,q,k,v,qh,kh,vh,cq,ck,cv,col,row,t,p,w,delta,s,do,dend,send)

def tables(beta,gains,seg,prev4):
    T=beta.shape[0]; n=T//CH
    ext=jnp.concatenate([prev4,seg])
    tri=(jnp.arange(CH)[:,None]>=jnp.arange(CH)[None,:]).astype(f32)
    cum=jnp.einsum("ts,csh->cth",tri,gains.reshape(n,CH,NH),precision=lax.Precision.HIGHEST)
    segc=seg.reshape(n,CH)
    prevc=jnp.concatenate([ext[2:3],segc[:-1,CH-1]])
    inn=(segc==prevc[:,None]).astype(f32)[:,:,None]*jnp.exp(cum)
    gam=(segc==segc[:,CH-1:])[:,:,None]
    gam=jnp.where(gam,jnp.exp(jnp.where(gam,cum[:,CH-1:]-cum,0.0)),0.0)
    cum=cum.reshape(T,NH); inn=inn.reshape(T,NH); gam=gam.reshape(T,NH)
    same=[(ext[3-j:3-j+T]==seg).astype(f32)[:,None] for j in range(1,CONV)]
    segf=seg.astype(f32)[:,None]
    def grp(g):
        sl=slice(g*HG,(g+1)*HG)
        pad=jnp.zeros((T,8-HG),f32)
        return jnp.concatenate([beta[:,sl],pad,cum[:,sl],pad,inn[:,sl],pad,gam[:,sl],pad,segf]+same+[jnp.zeros((T,64-36),f32)],1)
    col=jnp.stack([grp(g) for g in range(NH//HG)])
    cumT=cum.T
    row=jnp.stack([jnp.concatenate([cumT[g*HG:(g+1)*HG],jnp.zeros((8-HG,T),f32),segf.T,jnp.zeros((7,T),f32)],0) for g in range(NH//HG)])
    return col,row

TILES = 16640
MID = 6145 * 8
FFN_ROW = 8225 * 8 + 2
CLASSES = (
    (0, 2048, 1024, 8),
    (2048, 6144, 2049 * 1024, 16),
    (6144, 8192, 6177 * 1024 + 272, 8),
    (8192, 13824, 8226 * 1024 + 272, 22),
    (13824, 16640, 8226 * 1024 + 272 + 2 * D * FF, 8),
)
HALO = 240
EDGE = 32
MARGIN = 480
SMALL = 280
UNROLL = 4


def tile_loops(first, end, visit):
    for t0, t1, off, stride in CLASSES:
        lo = jnp.maximum(first, t0)
        hi = jnp.minimum(end, t1)

        @pl.loop(0, lax.div(jnp.maximum(hi - lo, 0) + (UNROLL - 1), UNROLL))
        def _(it):
            for u in range(UNROLL):
                t = jnp.minimum(lo + it * UNROLL + u, hi - 1)
                q = t - t0
                g = lax.div(q, stride)
                visit(off % 128 != 0, stride, t, off // 128 + g * (7 * stride) + q)


def repack_kernel(devices, pos, own, before, after, tiles, small, ext, shf):
    rows = own.shape[0]
    d = pos[0]
    per = TILES // devices
    ext[0:HALO] = before[...].astype(f32)
    ext[HALO : HALO + rows] = own[...]
    ext[HALO + rows : 2 * HALO + rows] = after[...].astype(f32)
    total = 2 * HALO + rows
    ext[total : total + 16] = jnp.zeros((16, 128), f32)
    lane = lax.broadcasted_iota(jnp.int32, (8, 128), 1)

    @pl.loop(0, (total + 7) // 8)
    def _(i):
        r = pl.multiple_of(i * 8, 8)
        a = pltpu.roll(ext[pl.ds(r, 8), :], 112, 1)
        b = pltpu.roll(ext[pl.ds(r + 1, 8), :], 112, 1)
        shf[pl.ds(r, 8), :] = jnp.where(lane < 112, a, b)

    base = d * rows - HALO

    def visit(shifted, stride, t, row):
        src = shf if shifted else ext
        tiles[t - d * per] = src[pl.ds(row - base, 8, stride=stride), :].astype(bf)

    tile_loops(d * per, d * per + per, visit)
    small[...] = jnp.zeros_like(small)
    for src, row, count, at in ((ext, 0, 8, 0), (ext, MID, 259, 8), (shf, FFN_ROW, 8, 272)):
        holder = row // rows
        assert (row + count - 1) // rows == holder

        @pl.when(d == holder)
        def _():
            s = row - holder * rows + HALO
            small[at : at + count] = src[s : s + count].astype(bf).astype(f32)


def repack(devices, pos, own, before, after):
    rows = own.shape[0]
    per = TILES // devices
    vm = pl.BlockSpec(memory_space=pltpu.VMEM)
    size = 2 * HALO + rows + 24
    return pl.pallas_call(
        lambda *refs: repack_kernel(devices, *refs),
        out_shape=[jax.ShapeDtypeStruct((per, 8, 128), bf), jax.ShapeDtypeStruct((SMALL, 128), f32)],
        in_specs=[pl.BlockSpec(memory_space=pltpu.SMEM), vm, vm, vm],
        out_specs=[vm, vm],
        scratch_shapes=[pltpu.VMEM((size, 128), f32), pltpu.VMEM((size, 128), f32)],
        cost_estimate=pl.CostEstimate(flops=0, bytes_accessed=4 * 2**20, transcendentals=0),
        name="repack",
    )(pos, own, before, after)


def unpack_kernel(devices, pos, own, before, after, small, flat, squares, ext, lin, shf):
    rows = flat.shape[0]
    d = pos[0]
    per = TILES // devices
    size = rows + 2 * MARGIN
    ext[0:EDGE] = before[...]
    ext[EDGE : EDGE + per] = own[...]
    ext[EDGE + per : 2 * EDGE + per] = after[...]
    shf[...] = jnp.zeros_like(shf)
    base = d * rows - MARGIN

    def visit(shifted, stride, t, row):
        dst = shf if shifted else lin
        dst[pl.ds(row - base, 8, stride=stride), :] = ext[t - d * per + EDGE].astype(f32)

    first = d * per
    tile_loops(jnp.maximum(first - EDGE, 0), jnp.minimum(first + per + EDGE, TILES), visit)
    for dst, row, count, at in ((lin, 0, 8, 0), (lin, MID, 258, 8), (shf, FFN_ROW, 8, 272)):
        holder = row // rows
        assert (row + count - 1) // rows == holder

        @pl.when(d == holder)
        def _():
            s = row - holder * rows + MARGIN
            dst[s : s + count] = small[at : at + count]

    tail = MID + 257
    holder = tail // rows
    lane8 = lax.broadcasted_iota(jnp.int32, (8, 128), 1)
    sub8 = lax.broadcasted_iota(jnp.int32, (8, 128), 0)

    @pl.when(d == holder)
    def _():
        s = tail - holder * rows + MARGIN
        moved = pltpu.roll(small[266:274], 112, 1)
        shf[s : s + 1] = jnp.where(lane8 >= 112, moved, shf[s : s + 8])[0:1]

    squares[...] = jnp.zeros_like(squares)

    def piece(r):
        a = pltpu.roll(shf[pl.ds(r + MARGIN, 8), :], 16, 1)
        b = pltpu.roll(shf[pl.ds(r + MARGIN - 1, 8), :], 16, 1)
        v = jnp.where(lane8 >= 16, a, b)
        return jnp.where(sub8 + (r + d * rows) < MID + 258, lin[pl.ds(r + MARGIN, 8), :], v)

    @pl.loop(0, rows // 8)
    def _(i):
        r = pl.multiple_of(i * 8, 8)
        v = piece(r)
        flat[pl.ds(r, 8), :] = v
        squares[...] += v * v

    left = rows % 8
    if left:
        r = rows - left
        v = jnp.where(sub8 < left, piece(r), 0.0)
        flat[r:rows] = v[0:left]
        squares[...] += v * v


def unpack(devices, pos, own, before, after, small):
    rows = NFLAT // 128 // devices
    per = TILES // devices
    vm = pl.BlockSpec(memory_space=pltpu.VMEM)
    size = rows + 2 * MARGIN + 8
    return pl.pallas_call(
        lambda *refs: unpack_kernel(devices, *refs),
        out_shape=[jax.ShapeDtypeStruct((rows, 128), f32), jax.ShapeDtypeStruct((8, 128), f32)],
        in_specs=[pl.BlockSpec(memory_space=pltpu.SMEM), vm, vm, vm, vm],
        out_specs=[vm, vm],
        scratch_shapes=[pltpu.VMEM((per + 2 * EDGE, 8, 128), bf), pltpu.VMEM((size, 128), f32), pltpu.VMEM((size, 128), f32)],
        cost_estimate=pl.CostEstimate(flops=0, bytes_accessed=4 * 2**20, transcendentals=0),
        name="unpack",
    )(pos, own, before, after, small)


PT = TILES // 128


def moves(fn):
    out = []
    for d in range(32):
        y, x, c, z = d // 16, d // 8 % 2, d // 4 % 2, d % 4
        y, x, c, z = fn(y, x, c, z)
        out.append((d, ((y * 2 + x) * 2 + c) * 4 + z))
    return out


TO_X = moves(lambda y, x, c, z: (y, 1 - x, c, z))
TO_Y = moves(lambda y, x, c, z: (1 - y, x, c, z))
TO_DIAG = moves(lambda y, x, c, z: (1 - y, 1 - x, c, z))
TO_CORE = moves(lambda y, x, c, z: (y, x, 1 - c, z))
UP = [moves(lambda y, x, c, z, s=s: (y, x, c, (z + s) % 4)) for s in range(4)]
DOWN = [moves(lambda y, x, c, z, s=s: (y, x, c, (z - s) % 4)) for s in range(4)]
PAIR_Z = moves(lambda y, x, c, z: (y, x, c, z ^ 1))


def send(v, pairs):
    return lax.ppermute(v, AXES, pairs)


def neighbours(first_rows, last_rows, devices):
    before = send(last_rows, [(i, i + 1) for i in range(devices - 1)])
    after = send(first_rows, [(i + 1, i) for i in range(devices - 1)])
    return before, after


def total_of(v, devices):
    if devices != 32:
        return lax.psum(v, AXES)
    for pairs in (TO_CORE, TO_X, TO_Y, PAIR_Z, UP[2]):
        v = v + send(v, pairs)
    return v


def spread(tiles, k):
    parts = tiles.reshape(4, PT, 8, 128)

    def part(i):
        return lax.dynamic_index_in_dim(parts, k ^ i, 0, False)

    got = jnp.stack([part(0), send(part(1), TO_X), send(part(2), TO_Y), send(part(3), TO_DIAG)])
    return [lax.dynamic_index_in_dim(got, k ^ i, 0, False) for i in range(4)]


def collect(pieces, k):
    stacked = jnp.stack(pieces)

    def piece(i):
        return lax.dynamic_index_in_dim(stacked, k ^ i, 0, False)

    got = jnp.stack([piece(0), send(piece(1), TO_X), send(piece(2), TO_Y), send(piece(3), TO_DIAG)])
    return jnp.stack([lax.dynamic_index_in_dim(got, k ^ i, 0, False) for i in range(4)]).reshape(4 * PT, 8, 128)


def gather_pieces(r):
    z1, z2, z3 = [send(r, UP[s]) for s in (1, 2, 3)]
    ca, cb = jnp.stack([r, z1]), jnp.stack([z2, z3])
    xa, yb = send(ca, TO_X), send(cb, TO_Y)
    xb, ya = send(cb, TO_X), send(ca, TO_Y)
    da, db = send(xa, TO_Y), send(yb, TO_X)
    own = [ca, cb, xa, xb, ya, yb, da, db]
    return own + [send(v, TO_CORE) for v in own]


def assemble_kernel(lead, pos, *refs):
    ins, rest = refs[:16], refs[16:]
    if lead:
        head, out, buf, hbuf, si, so, hsem = rest
        h_in = pltpu.make_async_copy(head.at[pl.ds(head.shape[0] - lead, lead)], hbuf, hsem.at[0])
        h_in.start()
    else:
        out, buf, si, so = rest
    k, c, z = pos[1], pos[2], pos[3]
    loads = [pltpu.make_async_copy(ins[a], buf.at[a], si.at[a]) for a in range(16)]
    for cp in loads:
        cp.start()
    stores = []
    for a in range(16):
        loads[a].wait()
        half = c if a < 8 else 1 - c
        for e in range(2):
            zz = lax.rem(z - (a % 2) * 2 - e + 4, 4)
            at = lead + ((half * 4 + zz) * 4 + (k ^ (a % 8 // 2))) * PT
            cp = pltpu.make_async_copy(buf.at[a, e], out.at[pl.ds(at, PT)], so.at[a * 2 + e])
            cp.start()
            stores.append(cp)
    if lead:
        h_in.wait()
        h_out = pltpu.make_async_copy(hbuf, out.at[pl.ds(0, lead)], hsem.at[1])
        h_out.start()
        h_out.wait()
    for cp in stores:
        cp.wait()


def assemble(pos, pieces, head=None, lead=0):
    hbm = pl.BlockSpec(memory_space=pl.ANY)
    scratch = [pltpu.VMEM((16, 2, PT, 8, 128), bf)] + ([pltpu.VMEM((lead, 8, 128), bf)] if lead else [])
    scratch += [pltpu.SemaphoreType.DMA((16,)), pltpu.SemaphoreType.DMA((32,))]
    scratch += [pltpu.SemaphoreType.DMA((2,))] if lead else []
    return pl.pallas_call(
        lambda *refs: assemble_kernel(lead, *refs),
        out_shape=jax.ShapeDtypeStruct((lead + 32 * PT, 8, 128), bf),
        in_specs=[pl.BlockSpec(memory_space=pltpu.SMEM)] + [hbm] * (16 + bool(lead)),
        out_specs=hbm,
        scratch_shapes=scratch,
        cost_estimate=pl.CostEstimate(flops=0, bytes_accessed=2 * 32 * PT * 2048, transcendentals=0),
        name="assemble",
    )(pos, *pieces, *([head] if lead else []))


def scatter_kernel(ranges, pos, *refs):
    ins, (own, oth, buf, si, so) = refs[: len(ranges)], refs[len(ranges) :]
    k, c, z = pos[1], pos[2], pos[3]
    loads = []
    at = 0
    cuts = []
    for ref, (first, count) in zip(ins, ranges):
        done = 0
        while done < count:
            step = min(count - done, PT - (at + done) % PT)
            cuts.append((ref, first + done, at + done, step))
            done += step
        at += count
    assert at == 32 * PT
    by_piece = [[] for _ in range(32)]
    for i, (ref, src, dst, step) in enumerate(cuts):
        cp = pltpu.make_async_copy(ref.at[pl.ds(src, step)], buf.at[pl.ds(dst, step)], si.at[i])
        cp.start()
        by_piece[dst // PT].append(cp)
    for p in range(32):
        for cp in by_piece[p]:
            cp.wait()
        half, zz, kk = p // 16, p // 4 % 4, p % 4
        slot = (k ^ kk) * 4 + lax.rem(z - zz + 4, 4)

        @pl.when(c == half)
        def _():
            pltpu.make_async_copy(buf.at[pl.ds(p * PT, PT)], own.at[slot], so.at[p]).start()

        @pl.when(c != half)
        def _():
            pltpu.make_async_copy(buf.at[pl.ds(p * PT, PT)], oth.at[slot], so.at[p]).start()

    for p in range(32):
        pltpu.make_async_copy(buf.at[pl.ds(p * PT, PT)], own.at[0], so.at[p]).wait()


def scatter_pieces(pos, grads, ranges):
    hbm = pl.BlockSpec(memory_space=pl.ANY)
    shape = jax.ShapeDtypeStruct((16, PT, 8, 128), bf)
    return pl.pallas_call(
        lambda *refs: scatter_kernel(ranges, *refs),
        out_shape=[shape, shape],
        in_specs=[pl.BlockSpec(memory_space=pltpu.SMEM)] + [hbm] * len(grads),
        out_specs=[hbm, hbm],
        scratch_shapes=[pltpu.VMEM((32 * PT, 8, 128), bf), pltpu.SemaphoreType.DMA((32 + len(grads),)), pltpu.SemaphoreType.DMA((32,))],
        cost_estimate=pl.CostEstimate(flops=0, bytes_accessed=2 * 32 * PT * 2048, transcendentals=0),
        name="scatter",
    )(pos, *grads)


def added(*parts):
    total = parts[0].astype(f32)
    for v in parts[1:]:
        total = total + v.astype(f32)
    return total.astype(bf)


def reduce_pieces(own, oth):
    got = send(oth, TO_CORE)
    ca, cb, xa, xb, ya, yb, da, db = [added(own[2 * b : 2 * b + 2], got[2 * b : 2 * b + 2]) for b in range(8)]
    xa = added(xa, send(da, TO_Y))
    yb = added(yb, send(db, TO_X))
    ca = added(ca, send(ya, TO_Y), send(xa, TO_X))
    cb = added(cb, send(xb, TO_X), send(yb, TO_Y))
    return added(ca[0], send(ca[1], DOWN[1]), send(cb[0], DOWN[2]), send(cb[1], DOWN[3]))


def as_matrix(tiles, first, rows, cols):
    part = tiles[first : first + rows * cols // 1024]
    return part.reshape(rows // 8, cols // 128, 8, 128).transpose(0, 2, 1, 3).reshape(rows, cols)


def as_tiles(matrix):
    rows, cols = matrix.shape
    return matrix.reshape(rows // 8, 8, cols // 128, 128).transpose(0, 2, 1, 3).reshape(rows * cols // 1024, 8, 128)


def product(a, b):
    return jnp.dot(a, b, preferred_element_type=f32)


def back_mul(a, b):
    return lax.dot_general(a, b, (((1,), (1,)), ((), ())), preferred_element_type=f32)


def outer_sum(a, b):
    return lax.dot_general(a, b, (((0,), (0,)), ((), ())), preferred_element_type=f32)


def outer_low(a, b):
    return as_tiles(outer_sum(a, b).astype(bf))


def rms_norm(r, w):
    return r * lax.rsqrt(jnp.mean(r * r, -1, keepdims=True) + EPS_NORM) * w


def swiglu(g, u):
    return jax.nn.silu(g) * u


def chain(start, maps, steps, pairs, transposed):
    eq = "hji,hjk->hik" if transposed else "hij,hjk->hik"
    v = send_shard(start, pairs)
    for _ in range(steps - 2):
        v = send_shard(jnp.einsum(eq, maps, v, precision=lax.Precision.HIGHEST) + start, pairs)
    return v


def send_shard(v, pairs):
    return lax.ppermute(v.astype(bf), "shard", pairs).astype(f32)


def local(inputs, cotangent, segments, master, moment_one, moment_two):
    shards = lax.axis_size("shard")
    devices = lax.axis_size("rep") * shards
    z = lax.axis_index("shard")
    rep = lax.axis_index("rep")
    T = inputs.shape[1]
    up = [(i, i + 1) for i in range(shards - 1)]
    down = [(i + 1, i) for i in range(shards - 1)]
    pos = jnp.stack([rep * shards + z, rep // 2, rep % 2, z]).astype(jnp.int32)
    k = rep // 2
    rows = NFLAT // 128 // devices
    master_rows = master.reshape(rows, 128)
    before, after = neighbours(master_rows[:HALO].astype(bf), master_rows[rows - HALO :].astype(bf), devices)
    tiles, small = repack(devices, pos, master_rows, before, after)
    if devices == 32:
        r = spread(tiles, k)
        q0 = assemble(pos, gather_pieces(r[0]))
        q1 = assemble(pos, gather_pieces(r[1]), q0, 64)
        q2 = assemble(pos, gather_pieces(r[2]), q1, 128)
        q3 = assemble(pos, gather_pieces(r[3]), q2, 1472)
        places = ((q0, 0), (q0, 1024), (q0, 2048), (q1, 0), (q1, 2048), (q2, 0), (q3, 0), (q3, 2816))
    else:
        everything = lax.all_gather(tiles, AXES, axis=0, tiled=True)
        places = [(everything, t) for t in (0, 1024, 2048, 4096, 6144, 8192, 11008, 13824)]
    sizes = ((D, 1024), (D, 1024), (D, 2048), (D, 2048), (2048, D), (D, FF), (D, FF), (FF, D))
    w_query, w_key, w_value, w_gate, w_out, w_ffgate, w_ffup, w_ffdown = [
        as_matrix(b, t, *s) for (b, t), s in zip(places, sizes)
    ]
    smalls = total_of(small, devices).reshape(-1)
    norm_in = smalls[:1024]
    mid = smalls[1024 : 1024 + 33040]
    w_decay = mid[:8192].reshape(D, NH)
    w_beta = mid[8192:16384].reshape(D, NH)
    decay_log = mid[16384:16392]
    decay_bias = mid[16392:16400]
    conv_query = mid[16400:20496].reshape(CONV, 1024)
    conv_key = mid[20496:24592].reshape(CONV, 1024)
    conv_value = mid[24592:32784].reshape(CONV, 2048)
    norm_head = jnp.broadcast_to(mid[32784:33040][None], (8, DV))
    norm_ffn = smalls[272 * 128 :]
    w_db = jnp.concatenate([w_decay, w_beta], 1).astype(bf)

    seg_pad = jnp.concatenate([jnp.full((CONV - 1,), -1, jnp.int32), segments[0]])
    ext_segs = lax.dynamic_slice_in_dim(seg_pad, z * T, T + CONV - 1, 0)
    in_rows = inputs[0].astype(f32)
    normed, norm_pull = jax.vjp(rms_norm, in_rows, norm_in)
    normed_low = normed.astype(bf)
    pq = product(normed_low, w_query).astype(bf)
    pk = product(normed_low, w_key).astype(bf)
    pv = product(normed_low, w_value).astype(bf)
    gate_raw = product(normed_low, w_gate)
    db_raw = product(normed_low, w_db)
    halo = lax.ppermute(jnp.concatenate([pq[T - 16 :], pk[T - 16 :], pv[T - 16 :]], 1), "shard", up)
    qh, kh, vh = halo[:, :1024], halo[:, 1024:2048], halo[:, 2048:]

    def scalars(raw, dlog, dbias):
        beta = jax.nn.sigmoid(raw[:, NH:])
        gains = -jnp.exp(dlog)[None] * jax.nn.softplus(raw[:, :NH] + dbias[None])
        return beta, gains

    (beta, gains), scalars_pull = jax.vjp(scalars, db_raw, decay_log, decay_bias)
    col, row = tables(beta, gains, ext_segs[CONV - 1 :], ext_segs[: CONV - 1])
    qn, kn, t, p, w, u, mloc, nloc = local_pass(
        pq, pk, pv, qh, kh, vh, conv_query, conv_key, conv_value, col, row
    )
    s_in = chain(nloc, mloc, shards, up, False)
    mixed, gated, delta, states = mix_pass(qn, kn, p, w, u, col, s_in, gate_raw, norm_head)
    s_end = jnp.einsum("hij,hjk->hik", mloc, s_in, precision=lax.Precision.HIGHEST) + nloc
    branch = product(gated, w_out)
    middle = in_rows + branch
    normed_two, norm_two_pull = jax.vjp(rms_norm, middle, norm_ffn)
    normed_two_low = normed_two.astype(bf)
    ff_gate = product(normed_two_low, w_ffgate)
    ff_up = product(normed_two_low, w_ffup)
    hidden, swiglu_pull = jax.vjp(swiglu, ff_gate, ff_up)
    hidden_low = hidden.astype(bf)
    out_rows = middle + product(hidden_low, w_ffdown)
    cot = cotangent[0]
    g_ffdown = outer_low(hidden_low, cot)
    d_ffgate, d_ffup = swiglu_pull(back_mul(cot, w_ffdown))
    d_ffgate, d_ffup = d_ffgate.astype(bf), d_ffup.astype(bf)
    g_ffgate = outer_low(normed_two_low, d_ffgate)
    g_ffup = outer_low(normed_two_low, d_ffup)
    d_normed_two = back_mul(d_ffgate, w_ffgate) + back_mul(d_ffup, w_ffup)
    d_middle_norm, g_norm_ffn = norm_two_pull(d_normed_two)
    d_middle = cot.astype(f32) + d_middle_norm
    d_branch = d_middle.astype(bf)
    g_out = outer_low(gated, d_branch)
    d_gated = back_mul(d_branch, w_out)
    d_mixed, d_gate, g_norm_head, e_loc = unmix_pass(d_gated, mixed, gate_raw, norm_head, qn, kn, p, w, col)
    d_end = chain(e_loc, mloc, shards, down, True)
    g_gate = outer_low(normed_low, d_gate)
    dq, dk, dv, bq, bk, bv, tq, tk, tv, gq, gk, gv, dcol = back_pass(
        pq, pk, pv, qh, kh, vh, conv_query, conv_key, conv_value, col, row, t, p, w, delta, states, d_mixed, d_end, s_end
    )
    returned = lax.ppermute(jnp.concatenate([bq, bk, bv], 1), "shard", down)
    dq = dq.at[T - 8 :].set((tq + returned[:, :1024]).astype(bf))
    dk = dk.at[T - 8 :].set((tk + returned[:, 1024:2048]).astype(bf))
    dv = dv.at[T - 8 :].set((tv + returned[:, 2048:]).astype(bf))
    d_beta = jnp.concatenate([dcol[g][:, :HG] for g in range(NH // HG)], 1)
    d_cum = jnp.concatenate([dcol[g][:, HG : 2 * HG] for g in range(NH // HG)], 1)
    tri = (jnp.arange(CH)[:, None] <= jnp.arange(CH)[None, :]).astype(f32)
    d_gains = jnp.einsum("ts,csh->cth", tri, d_cum.reshape(T // CH, CH, NH), precision=lax.Precision.HIGHEST)
    d_raw, g_decay_log, g_decay_bias = scalars_pull((jnp.zeros_like(beta), d_gains.reshape(T, NH)))
    d_raw = (d_raw + jnp.concatenate([jnp.zeros_like(d_beta), d_beta], 1)).astype(bf)
    g_query = outer_low(normed_low, dq)
    g_key = outer_low(normed_low, dk)
    g_value = outer_low(normed_low, dv)
    g_db = outer_sum(normed_low, d_raw)
    d_normed = back_mul(dq, w_query) + back_mul(dk, w_key) + back_mul(dv, w_value) + back_mul(d_gate, w_gate)
    d_normed = d_normed + back_mul(d_raw, w_db)
    d_in_norm, g_norm_in = norm_pull(d_normed)
    d_inputs = (d_middle + d_in_norm).astype(bf)
    zeros = jnp.zeros
    small_grads = jnp.concatenate(
        [g_norm_in, g_db[:, :NH].reshape(-1), g_db[:, NH:].reshape(-1), g_decay_log, g_decay_bias]
        + [gq[:CONV].reshape(-1), gk[:CONV].reshape(-1), gv[:CONV].reshape(-1), jnp.sum(g_norm_head, 0)]
        + [zeros((112 + 640,), f32), g_norm_ffn]
    ).reshape(SMALL, 128)
    small_sum = total_of(small_grads, devices)
    if devices == 32:
        r3 = reduce_pieces(*scatter_pieces(pos, (g_ffup, g_ffdown), ((1472, 1344), (0, 2816))))
        r2 = reduce_pieces(*scatter_pieces(pos, (g_ffgate, g_ffup), ((128, 2688), (0, 1472))))
        r1 = reduce_pieces(*scatter_pieces(pos, (g_gate, g_out, g_ffgate), ((64, 1984), (0, 2048), (0, 128))))
        r0 = reduce_pieces(
            *scatter_pieces(pos, (g_query, g_key, g_value, g_gate), ((0, 1024), (0, 1024), (0, 2048), (0, 64)))
        )
        owned_tiles = collect([r0, r1, r2, r3], k)
    else:
        parts = [g_query, g_key, g_value, g_gate, g_out, g_ffgate, g_ffup, g_ffdown]
        owned_tiles = lax.psum_scatter(jnp.concatenate(parts), AXES, scatter_dimension=0, tiled=True)
    per = TILES // devices
    before, after = neighbours(owned_tiles[:EDGE], owned_tiles[per - EDGE :], devices)
    owned_rows, squares = unpack(devices, pos, owned_tiles, before, after, small_sum)
    owned = owned_rows.reshape(-1)
    grad_norm = jnp.sqrt(total_of(jnp.sum(squares), devices))
    clip_scale = jnp.minimum(1.0, math.sqrt(PARAMS) / (grad_norm + 1e-06))
    clipped = owned * clip_scale
    new_one = BETA_ONE * moment_one + (1.0 - BETA_ONE) * clipped
    new_two = BETA_TWO * moment_two + (1.0 - BETA_TWO) * clipped * clipped
    fix_one = 1.0 - BETA_ONE**STEP
    fix_two = 1.0 - BETA_TWO**STEP
    update = -LEARN_RATE * (new_one / fix_one / (jnp.sqrt(new_two / fix_two) + ADAM_EPS) + DECAY_RATE * master)
    output = out_rows.astype(bf)[None]
    return (output, d_inputs[None], owned, new_one, new_two, update, grad_norm)


def solution(mesh):
    flat = P(AXES)
    rows = P("rep", "shard", None)
    return jax.shard_map(
        local,
        mesh=mesh,
        in_specs=(rows, rows, P("rep", None), flat, flat, flat),
        out_specs=(rows, rows, flat, flat, flat, flat, P()),
        check_vma=False,
    )
```
